256 devices in a mesh: pts: 256 (over y, x, z, core).
Axes of the slice: x: 4, y: 4, z: 8, core: 2. Of those that a mesh axis runs over, the one named last changes fastest.
Arguments:
- rhs: float32 [64, 262144], P(None, 'pts'), may hold values from -6 to 6
- ridge: float32 [262144], P('pts'), may hold values from 0.1 to 2
- leaf_basis: float32 [1024, 256, 256], P('pts'), may hold values from -0.375 to 0.375
- leaf_transfer: float32 [1024, 256, 256], P('pts'), may hold values from -0.1875 to 0.1875
- near_blocks: float32 [1024, 3, 256, 256], P('pts'), may hold values from -0.375 to 0.375
- near_list: int32 [1024, 3], P('pts'), may hold values from 0 to 1023, as said below
- leaf_coupling: float32 [1024, 4, 256, 256], P('pts'), may hold values from -0.1875 to 0.1875
- leaf_far: int32 [1024, 4], P('pts'), may hold values from 0 to 1023, as said below
- node_coupling: float32 [256, 6, 256, 256], P('pts'), may hold values from -0.15625 to 0.15625
- node_far: int32 [256, 6], P('pts'), may hold values from 0 to 255, as said below
Outputs:
- product: float32 [64, 262144], P(None, 'pts')
The draws below stay inside these ranges and needn't reach their ends.
Inputs may be any that keep to these rules, and one draw needn't show every extreme that they name: `near_list`: entry 0 of each row is the leaf itself; the others are leaves 1 to 4 places away from it. `leaf_far`: leaves 1 to 4 places away from the row's leaf. `node_far`: First-level nodes 2 to 4 places away from the row's node; entries may repeat in rows near the ends.
All inputs are finite; a program needn't handle non-finite values.
Results may differ from the reference program's by a relative error of at most 0.000054.
Values sent between devices are 32-bit elements; how exact they have to be, the bound alone decides.
A program may use at most 64 MiB of HBM per device.

```python
import math
import jax
import jax.numpy as jnp
from jax import lax

LEAF = 256
RANK = 256
COLS = 64
RADIX = 4
NEAR = 3
FAR0 = 4
REACH1 = 4
FAR1 = 6
LEAVES_DEV = 4
LEAVES = 1024
NODES1 = 256
POINTS = 262144


def offsets_row(subkey, max_reach, how_many, nearest):
    span_size = max_reach - nearest + 1
    chosen = jax.random.permutation(subkey, 2 * span_size)[:how_many]
    return jnp.where(chosen < span_size, chosen - max_reach, chosen - span_size + nearest)


def reflect_rows(subkey, row_count, max_reach, how_many, nearest):
    subkeys = jax.random.split(subkey, row_count)
    offsets = jax.vmap(lambda single: offsets_row(single, max_reach, how_many, nearest))(subkeys)
    anchor = jnp.arange(row_count, dtype=jnp.int32)[:, None]
    shifted = anchor + offsets
    inside = (shifted >= 0) & (shifted < row_count)
    return jnp.where(inside, shifted, anchor - offsets).astype(jnp.int32)


def leaf_lists(key):
    return reflect_rows(jax.random.fold_in(key, 11), LEAVES, LEAVES_DEV, NEAR - 1 + FAR0, 1)


def draw_near_list(key, part):
    listed = leaf_lists(key)
    itself = jnp.arange(LEAVES, dtype=jnp.int32)[:, None]
    return jnp.concatenate([itself, listed[:, :NEAR - 1]], axis=1)


def draw_leaf_far(key, part):
    return leaf_lists(key)[:, NEAR - 1:]


def draw_node_far(key, part):
    return reflect_rows(jax.random.fold_in(key, 23), NODES1, REACH1, FAR1, 2)


def level_of(own_key, extent, cuts, low, largest):
    loudness = 1.0
    for axis_at, parts in cuts:
        draws = jax.random.uniform(jax.random.fold_in(jax.random.fold_in(own_key, 6), axis_at), (parts,), jnp.float32, low / len(cuts), largest / len(cuts))
        loudness = loudness * jnp.repeat(jnp.exp(draws), extent[axis_at] // parts).reshape((-1,) + (1,) * (len(extent) - 1 - axis_at))
    return loudness


def bell_draw(key, dims, deviation, reach, pieces=(), kind=jnp.bfloat16):
    gain = level_of(key, dims, pieces, -0.22, 0.18) if pieces else 1.0
    values = jax.random.normal(key, dims, jnp.float32) * deviation * gain
    return jnp.minimum(jnp.maximum(values, -reach), reach).astype(kind)


def setup_inputs(seed: int = 0) -> dict:
    arg_keys = jax.random.split(jax.random.key(seed), 11)
    return {
        "rhs": bell_draw(arg_keys[0], (COLS, POINTS), 1.0, 6.0, ((1, 256),), jnp.float32),
        "ridge": jnp.clip(jnp.exp(math.log(2.0) - 2.9957323 * jax.random.uniform(arg_keys[1], (POINTS,), jnp.float32) ** level_of(arg_keys[1], (POINTS,), ((0, 256),), -0.2, 0.2)), 0.1, 2.0),
        "leaf_basis": bell_draw(arg_keys[2], (LEAVES, LEAF, RANK), LEAF ** -0.5, 0.375, ((0, 256),), jnp.float32),
        "leaf_transfer": bell_draw(arg_keys[3], (LEAVES, RANK, RANK), (RADIX * RANK) ** -0.5, 0.1875, ((0, 256),), jnp.float32),
        "near_blocks": bell_draw(arg_keys[4], (LEAVES, NEAR, LEAF, LEAF), LEAF ** -0.5, 0.375, ((0, 256),), jnp.float32),
        "near_list": draw_near_list(jax.random.fold_in(arg_keys[10], 71), 0),
        "leaf_coupling": bell_draw(arg_keys[6], (LEAVES, FAR0, RANK, RANK), (FAR0 * RANK) ** -0.5, 0.1875, ((0, 256),), jnp.float32),
        "leaf_far": draw_leaf_far(jax.random.fold_in(arg_keys[10], 71), 0),
        "node_coupling": bell_draw(arg_keys[8], (NODES1, FAR1, RANK, RANK), (FAR1 * RANK) ** -0.5, 0.15625, ((0, 256),), jnp.float32),
        "node_far": draw_node_far(jax.random.fold_in(arg_keys[10], 71), 0),
    }


highest = lax.Precision.HIGHEST


def reference(rhs, ridge, leaf_basis, leaf_transfer, near_blocks, near_list, leaf_coupling, leaf_far, node_coupling, node_far):
    columns = rhs.shape[0]
    leaf_rhs = rhs.reshape(columns, LEAVES, LEAF)
    moments = jnp.einsum("clp,lpr->lcr", leaf_rhs, leaf_basis, precision=highest)
    lifted = jnp.einsum("lcr,lrs->lcs", moments, leaf_transfer, precision=highest)
    node_moment = lifted.reshape(NODES1, RADIX, columns, RANK).sum(axis=1)
    leaf_field = jnp.einsum("lkcr,lkrs->lcs", jnp.take(moments, leaf_far, axis=0), leaf_coupling, precision=highest)
    node_field = jnp.einsum("nkcr,nkrs->ncs", jnp.take(node_moment, node_far, axis=0), node_coupling, precision=highest)
    leaf_total = leaf_field + jnp.einsum("lcs,lrs->lcr", jnp.repeat(node_field, RADIX, axis=0), leaf_transfer, precision=highest)
    far_part = jnp.einsum("lcr,lpr->clp", leaf_total, leaf_basis, precision=highest)
    near_points = jnp.take(leaf_rhs, near_list, axis=1)
    near_part = jnp.einsum("cljp,ljpq->clq", near_points, near_blocks, precision=highest)
    product = (far_part + near_part).reshape(columns, POINTS) + ridge[None, :] * rhs
    return product
```

```python
import jax
import jax.numpy as jnp
from jax import lax
from jax.experimental import pallas as pl
from jax.experimental.pallas import tpu as pltpu
from jax.sharding import PartitionSpec as P

F32 = jnp.float32
BF16 = jnp.bfloat16
MESH = pl.DeviceIdType.MESH


def split(value):
    high = value.astype(BF16)
    low = (value - high.astype(F32)).astype(BF16)
    return high, low


def stacked(value):
    high, low = split(value)
    return jnp.concatenate([high, low], axis=0)


def product(left, weight, transposed=False):
    rows = left.shape[0] // 2
    high, low = split(weight)
    dims = (((1,), (1 if transposed else 0,)), ((), ()))
    both = lax.dot_general(left, high, dims, preferred_element_type=F32)
    rest = lax.dot_general(left[:rows], low, dims, preferred_element_type=F32)
    return both[:rows] + (both[rows:] + rest)


def inside(index, extent):
    return jnp.minimum(jnp.maximum(index, 0), extent - 1)


def kernel(
    count,
    rhs,
    basis_hbm,
    transfer_hbm,
    near_hbm,
    near_list_hbm,
    coupling_hbm,
    leaf_far_hbm,
    node_coupling_hbm,
    node_far_hbm,
    out,
    x_window,
    m_window,
    n_own,
    n_window,
    basis,
    transfer,
    near,
    coupling,
    node_coupling,
    near_list,
    leaf_far,
    node_far,
    load_sem,
    list_sem,
    send_sem,
    recv_sem,
):
    leaves = basis.shape[0]
    size = basis.shape[1]
    me = lax.axis_index("pts")
    parity = lax.rem(me, 2)
    right = lax.rem(me + 1, count)
    left = lax.rem(me + count - 1, count)
    right2 = lax.rem(me + 2, count)
    left2 = lax.rem(me + count - 2, count)
    partner = me + 1 - 2 * parity
    first = me * leaves - leaves

    def cols(l):
        return slice(l * size, (l + 1) * size)

    barrier = pltpu.get_barrier_semaphore()
    for other in (left, right, left2, right2):
        pl.semaphore_signal(barrier, inc=1, device_id=(other,), device_id_type=MESH)

    loads = {}

    def load(name, source, target, slot):
        copy = pltpu.make_async_copy(source, target, load_sem.at[slot])
        copy.start()
        loads[name] = copy

    slot = 0
    for l in range(leaves):
        load(("x", l), rhs.at[:, cols(l)], x_window.at[leaves + l], slot)
        load(("b", l), basis_hbm.at[l], basis.at[l], slot + 1)
        slot += 2
    for l in range(leaves):
        load(("t", l), transfer_hbm.at[l], transfer.at[l], slot)
        slot += 1
    lists = [
        pltpu.make_async_copy(near_list_hbm, near_list, list_sem.at[0]),
        pltpu.make_async_copy(leaf_far_hbm, leaf_far, list_sem.at[1]),
        pltpu.make_async_copy(node_far_hbm, node_far, list_sem.at[2]),
    ]
    for copy in lists:
        copy.start()
    for l in range(leaves):
        load(("n", l), near_hbm.at[l], near.at[l], slot)
        slot += 1
    load(("k", 0), node_coupling_hbm.at[0], node_coupling, slot)
    slot += 1
    for l in range(leaves):
        load(("c", l), coupling_hbm.at[l], coupling.at[l], slot)
        slot += 1

    pl.semaphore_wait(barrier, 4)

    def send(source, target, number, device):
        copy = pltpu.make_async_remote_copy(
            src_ref=source,
            dst_ref=target,
            send_sem=send_sem.at[number],
            recv_sem=recv_sem.at[number],
            device_id=(device,),
            device_id_type=MESH,
        )
        copy.start()
        return copy

    x_copies = []
    for i in range(leaves):
        a = leaves - 1 - i
        x_copies.append(send(rhs.at[:, cols(a)], x_window.at[a], 2 * i, right))
        x_copies.append(
            send(rhs.at[:, cols(i)], x_window.at[2 * leaves + i], 2 * i + 1, left)
        )

    node = None
    for l in range(leaves):
        loads["x", l].wait()
        loads["b", l].wait()
        moment = product(stacked(x_window[leaves + l]), basis[l])
        m_window[leaves + l] = moment
        loads["t", l].wait()
        term = product(stacked(moment), transfer[l])
        node = term if node is None else node + term
    n_own[...] = node

    base = 2 * leaves
    n_right = send(n_own, n_window.at[2], base, right2)
    n_left = send(n_own, n_window.at[3], base + 1, left2)
    base += 2
    m_copies = []
    for i in range(leaves):
        a = leaves - 1 - i
        m_copies.append(send(m_window.at[leaves + a], m_window.at[a], base + 2 * i, right))
        m_copies.append(
            send(m_window.at[leaves + i], m_window.at[2 * leaves + i], base + 2 * i + 1, left)
        )
    base += 2 * leaves

    for l in range(leaves):
        loads["n", l].wait()
        out[:, cols(l)] = product(stacked(x_window[leaves + l]), near[l, 0])

    n_right.wait_recv()
    n_left.wait_recv()
    relay_right = send(n_window.at[2], n_window.at[0], base, right2)
    relay_left = send(n_window.at[3], n_window.at[5], base + 1, left2)
    across = send(n_window.at[2 + parity], n_window.at[1 + 3 * parity], base + 2, partner)
    base += 3

    for copy in x_copies:
        copy.wait_recv()
    for copy in lists:
        copy.wait()
    for l in range(leaves):
        total = out[:, cols(l)]
        for j in range(1, near.shape[1]):
            source = inside(near_list[l, j] - first, 3 * leaves)
            total = total + product(stacked(x_window[source]), near[l, j])
        out[:, cols(l)] = total

    relay_right.wait_recv()
    relay_left.wait_recv()
    across2 = send(n_window.at[5 - 5 * parity], n_window.at[4 - 3 * parity], base, partner)
    loads["k", 0].wait()
    across.wait_recv()
    across2.wait_recv()
    field = None
    for k in range(node_coupling.shape[0]):
        offset = node_far[0, k] - me
        source = inside(jnp.where(offset < 0, offset + 4, offset + 1), 6)
        term = product(stacked(n_window[source]), node_coupling[k])
        field = term if field is None else field + term
    field = stacked(field)

    for copy in m_copies:
        copy.wait_recv()
    for l in range(leaves):
        loads["c", l].wait()
        total = product(field, transfer[l], transposed=True)
        for k in range(coupling.shape[1]):
            source = inside(leaf_far[l, k] - first, 3 * leaves)
            total = total + product(stacked(m_window[source]), coupling[l, k])
        out[:, cols(l)] = out[:, cols(l)] + product(stacked(total), basis[l], transposed=True)

    for copy in x_copies + m_copies + [n_right, n_left, relay_right, relay_left, across, across2]:
        copy.wait_send()


def per_device(
    rhs,
    ridge,
    leaf_basis,
    leaf_transfer,
    near_blocks,
    near_list,
    leaf_coupling,
    leaf_far,
    node_coupling,
    node_far,
):
    leaves, size, rank = leaf_basis.shape
    columns = rhs.shape[0]
    count = lax.axis_size("pts")
    in_hbm = pl.BlockSpec(memory_space=pltpu.HBM)
    vmem = pl.BlockSpec(memory_space=pltpu.VMEM)
    copies = 4 * leaves + 6
    result = pl.pallas_call(
        lambda *refs: kernel(count, *refs),
        out_shape=jax.ShapeDtypeStruct((columns, leaves * size), F32),
        in_specs=[in_hbm] * 9,
        out_specs=vmem,
        scratch_shapes=[
            pltpu.VMEM((3 * leaves, columns, size), F32),
            pltpu.VMEM((3 * leaves, columns, rank), F32),
            pltpu.VMEM((columns, rank), F32),
            pltpu.VMEM((6, columns, rank), F32),
            pltpu.VMEM(leaf_basis.shape, F32),
            pltpu.VMEM(leaf_transfer.shape, F32),
            pltpu.VMEM(near_blocks.shape, F32),
            pltpu.VMEM(leaf_coupling.shape, F32),
            pltpu.VMEM(node_coupling.shape[1:], F32),
            pltpu.SMEM(near_list.shape, jnp.int32),
            pltpu.SMEM(leaf_far.shape, jnp.int32),
            pltpu.SMEM(node_far.shape, jnp.int32),
            pltpu.SemaphoreType.DMA((5 * leaves + 1,)),
            pltpu.SemaphoreType.DMA((3,)),
            pltpu.SemaphoreType.DMA((copies,)),
            pltpu.SemaphoreType.DMA((copies,)),
        ],
        compiler_params=pltpu.CompilerParams(
            collective_id=0, has_side_effects=True, vmem_limit_bytes=66486272
        ),
    )(
        rhs,
        leaf_basis,
        leaf_transfer,
        near_blocks,
        near_list,
        leaf_coupling,
        leaf_far,
        node_coupling,
        node_far,
    )
    return result + ridge[None, :] * rhs


def solution(mesh):
    in_specs = (
        P(None, "pts"),
        P("pts"),
        P("pts", None, None),
        P("pts", None, None),
        P("pts", None, None, None),
        P("pts", None),
        P("pts", None, None, None),
        P("pts", None),
        P("pts", None, None, None),
        P("pts", None),
    )
    return jax.shard_map(
        per_device, mesh=mesh, in_specs=in_specs, out_specs=P(None, "pts"), check_vma=False
    )
```

```python
import jax
import jax.numpy as jnp
from jax import lax
from jax.experimental import pallas as pl
from jax.experimental.pallas import tpu as pltpu
from jax.sharding import PartitionSpec as P

F32 = jnp.float32
BF16 = jnp.bfloat16
MESH = pl.DeviceIdType.MESH

COLUMN = 16


def split(value):
    high = value.astype(BF16)
    low = (value - high.astype(F32)).astype(BF16)
    return high, low


def stacked(value):
    high, low = split(value)
    return jnp.concatenate([high, low], axis=0)


def halves(left, high, low, transposed=False):
    rows = left.shape[0] // 2
    dims = (((1,), (1 if transposed else 0,)), ((), ()))
    both = lax.dot_general(left, high, dims, preferred_element_type=F32)
    rest = lax.dot_general(left[:rows], low, dims, preferred_element_type=F32)
    return both[:rows] + (both[rows:] + rest)


def product(left, weight):
    return halves(left, *split(weight))


def inside(index, extent):
    return jnp.minimum(jnp.maximum(index, 0), extent - 1)


def flag(condition):
    return condition.astype(jnp.int32).astype(F32)


def kernel(
    count,
    rhs,
    basis_hbm,
    transfer_hbm,
    near_hbm,
    near_list_hbm,
    coupling_hbm,
    leaf_far_hbm,
    node_coupling_hbm,
    node_far_hbm,
    out,
    x_window,
    x_last,
    m_window,
    m_last,
    n_own,
    n_window,
    field_sum,
    basis,
    transfer,
    near,
    coupling,
    node_coupling,
    basis_parts,
    transfer_parts,
    last_parts,
    node_parts,
    near_list,
    leaf_far,
    node_far,
    load_sem,
    send_sem,
    recv_sem,
):
    leaves, size = basis.shape[:2]
    inner = 3 * leaves - 2
    me = lax.axis_index("pts")
    parity = lax.rem(me, 2)
    chip = me // 2
    chips = count // 2
    even = parity == 0
    odd = parity == 1
    has_left = me >= 1
    has_right = me < count - 1
    near_chip_left = chip >= 1
    near_chip_right = chip < chips - 1
    far_chip_left = chip >= 2
    far_chip_right = chip < chips - 2
    right = jnp.minimum(me + 1, count - 1)
    left = jnp.maximum(me - 1, 0)
    right2 = jnp.minimum(me + 2, count - 1)
    left2 = jnp.maximum(me - 2, 0)
    right_first = lax.rem(me, COLUMN) < 4
    partner = me + 1 - 2 * parity
    first = me * leaves - leaves

    def cols(l):
        return slice(l * size, (l + 1) * size)

    barrier = pltpu.get_barrier_semaphore()
    expected = 0
    for other, there in (
        (left, has_left),
        (right, has_right),
        (left2, near_chip_left),
        (right2, near_chip_right),
    ):
        expected = expected + there.astype(jnp.int32)

        @pl.when(there)
        def _(other=other):
            pl.semaphore_signal(barrier, inc=1, device_id=(other,), device_id_type=MESH)

    def load(source, target, number):
        copy = pltpu.make_async_copy(source, target, load_sem.at[number])
        copy.start()
        return copy

    x_loads = [load(rhs.at[:, cols(l)], x_window.at[leaves - 1 + l], l) for l in range(leaves)]
    basis_loads = [load(basis_hbm.at[l], basis.at[l], leaves + l) for l in range(leaves)]
    transfer_loads = [
        load(transfer_hbm.at[l], transfer.at[l], 2 * leaves + l) for l in range(leaves)
    ]
    base = 3 * leaves
    list_loads = [
        load(near_list_hbm, near_list, base),
        load(leaf_far_hbm, leaf_far, base + 1),
        load(node_far_hbm, node_far, base + 2),
    ]
    node_load = load(node_coupling_hbm.at[0], node_coupling, base + 5)
    near_load = load(near_hbm, near, base + 3)
    coupling_load = load(coupling_hbm, coupling, base + 4)

    pl.semaphore_wait(barrier, expected)

    def remote(source, target, number, device):
        return pltpu.make_async_remote_copy(
            src_ref=source,
            dst_ref=target,
            send_sem=send_sem.at[number],
            recv_sem=recv_sem.at[number],
            device_id=(device,),
            device_id_type=MESH,
        )

    end = leaves - 1
    x_right = [
        remote(rhs.at[:, cols(l)], x_window.at[l - 1], 11 + l, right) for l in range(end, 0, -1)
    ]
    x_left = [
        remote(rhs.at[:, cols(l)], x_window.at[2 * leaves - 1 + l], 11 + leaves + l, left)
        for l in range(end)
    ]
    m_right = remote(m_window.at[leaves : 2 * leaves - 1], m_window.at[0:end], 2, right)
    m_left = remote(m_window.at[end : 2 * end], m_window.at[2 * leaves - 1 : inner], 3, left)
    m_last_right = remote(m_window.at[end], m_last.at[0], 4, right)
    m_last_left = remote(m_window.at[2 * end], m_last.at[1], 5, left)
    x_last_right = remote(rhs.at[:, cols(0)], x_last.at[0], 6, right)
    x_last_left = remote(rhs.at[:, cols(end)], x_last.at[1], 7, left)
    n_right = remote(n_own, n_window.at[2], 8, right2)
    n_left = remote(n_own, n_window.at[3], 9, left2)
    relay_right = remote(n_window.at[2], n_window.at[0], 10, right2)
    relay_left = remote(n_window.at[3], n_window.at[5], 11, left2)
    low_early = remote(n_window.at[2], n_window.at[1], 0, partner)
    low_late = remote(n_window.at[0], n_window.at[1], 0, partner)
    high_early = remote(n_window.at[3], n_window.at[4], 1, partner)
    high_late = remote(n_window.at[5], n_window.at[4], 1, partner)

    def if_start(condition, *copies):
        @pl.when(condition)
        def _():
            for copy in copies:
                copy.start()

    def if_arrived(condition, *copies):
        @pl.when(condition)
        def _():
            for copy in copies:
                copy.wait_recv()

    if_start(has_right, *x_right)
    if_start(has_left, *x_left)

    node = None
    for l in range(leaves):
        x_loads[l].wait()
        basis_loads[l].wait()
        high, low = split(basis[l])
        basis_parts[l, 0] = high
        basis_parts[l, 1] = low
        moment = halves(stacked(x_window[end + l]), high, low)
        m_window[end + l] = moment
        transfer_loads[l].wait()
        high, low = split(transfer[l])
        transfer_parts[l, 0] = high
        transfer_parts[l, 1] = low
        term = halves(stacked(moment), high, low)
        node = term if node is None else node + term
    n_own[...] = node

    if_start(near_chip_right, n_right)
    if_start(near_chip_left, n_left)
    if_start(has_right, m_right)
    if_start(has_left, m_left)

    for copy in list_loads:
        copy.wait()
    node_load.wait()
    entries = node_coupling.shape[0]
    for s, offset in enumerate((-4, -3, -2, 2, 3, 4)):
        total = None
        for k in range(entries):
            term = flag(node_far[0, k] == me + offset) * node_coupling[k]
            total = term if total is None else total + term
        node_parts[s, 0], node_parts[s, 1] = split(total)

    for l in range(leaves):
        left_parts = jnp.concatenate([basis_parts[l, 0], basis_parts[l, 1]], axis=0)
        both = halves(left_parts, transfer_parts[l, 0], transfer_parts[l, 1])
        transfer_parts[l, 0], transfer_parts[l, 1] = split(both)

    near_load.wait()
    for l in range(leaves):
        out[:, cols(l)] = product(stacked(x_window[end + l]), near[l, 0])

    def from_left():
        @pl.when(near_chip_left)
        def _():
            n_right.wait_recv()
            if_start(near_chip_right, relay_right)
            if_start(even, low_early)

        if_start(has_right, m_last_right, x_last_right)

    def from_right():
        @pl.when(near_chip_right)
        def _():
            n_left.wait_recv()
            if_start(near_chip_left, relay_left)
            if_start(odd, high_early)

        if_start(has_left, m_last_left, x_last_left)

    def in_order(one, other):
        @pl.when(right_first)
        def _():
            other()
            one()

        @pl.when(jnp.logical_not(right_first))
        def _():
            one()
            other()

    in_order(from_left, from_right)

    coupling_load.wait()
    ends = ((0, 0, first), (1, end, first + 3 * leaves - 1))
    for side, l, source in ends:
        total = flag(near_list[l, 1] == source) * near[l, 1]
        for j in range(2, near.shape[1]):
            total = total + flag(near_list[l, j] == source) * near[l, j]
        last_parts[side, 0], last_parts[side, 1] = split(total)
        total = flag(leaf_far[l, 0] == source) * coupling[l, 0]
        for k in range(1, coupling.shape[1]):
            total = total + flag(leaf_far[l, k] == source) * coupling[l, k]
        last_parts[side, 2], last_parts[side, 3] = split(total)

    def chosen(window, leaf, l):
        slot = leaf - first - 1
        value = window[inside(slot, inner)]
        if l == 0:
            value = value * flag(slot >= 0)
        if l == end:
            value = value * flag(slot < inner)
        return stacked(value)

    if_arrived(has_left, *x_right)
    if_arrived(has_right, *x_left)
    for l in range(leaves):
        total = out[:, cols(l)]
        for j in range(1, near.shape[1]):
            total = total + product(chosen(x_window, near_list[l, j], l), near[l, j])
        out[:, cols(l)] = total

    if_arrived(has_left, m_right)
    if_arrived(has_right, m_left)
    for l in range(leaves):
        total = None
        for k in range(coupling.shape[1]):
            term = product(chosen(m_window, leaf_far[l, k], l), coupling[l, k])
            total = term if total is None else total + term
        total = halves(stacked(total), basis_parts[l, 0], basis_parts[l, 1], True)
        out[:, cols(l)] = out[:, cols(l)] + total

    def node_term(s, there):
        value = stacked(jnp.where(there, n_window[s], 0.0))
        return halves(value, node_parts[s, 0], node_parts[s, 1])

    field_sum[...] = node_term(2, near_chip_left) + node_term(3, near_chip_right)

    def later_left():
        @pl.when(far_chip_left)
        def _():
            relay_right.wait_recv()
            if_start(odd, low_late)

    def later_right():
        @pl.when(far_chip_right)
        def _():
            relay_left.wait_recv()
            if_start(even, high_late)

    in_order(later_left, later_right)
    field_sum[...] = (
        field_sum[...] + node_term(0, far_chip_left) + node_term(5, far_chip_right)
    )

    if_arrived(has_left, m_last_right)
    if_arrived(has_right, m_last_left)

    def last(buffer, side):
        return stacked(jnp.where((has_left, has_right)[side], buffer[side], 0.0))

    for side, l in ((0, 0), (1, end)):
        total = halves(last(m_last, side), last_parts[side, 2], last_parts[side, 3])
        total = halves(stacked(total), basis_parts[l, 0], basis_parts[l, 1], True)
        out[:, cols(l)] = out[:, cols(l)] + total

    low_there = chip >= 2 - parity
    high_there = chip < chips - 1 - parity
    if_arrived(low_there, low_early)
    if_arrived(high_there, high_early)
    field = stacked(field_sum[...] + node_term(1, low_there) + node_term(4, high_there))
    for l in range(leaves):
        term = halves(field, transfer_parts[l, 0], transfer_parts[l, 1], True)
        out[:, cols(l)] = out[:, cols(l)] + term

    if_arrived(has_left, x_last_right)
    if_arrived(has_right, x_last_left)
    for side, l in ((0, 0), (1, end)):
        parts = last_parts[side, 0], last_parts[side, 1]
        out[:, cols(l)] = out[:, cols(l)] + halves(last(x_last, side), *parts)

    def if_sent(condition, *copies):
        @pl.when(condition)
        def _():
            for copy in copies:
                copy.wait_send()

    if_sent(has_right, *x_right, m_right, m_last_right, x_last_right)
    if_sent(has_left, *x_left, m_left, m_last_left, x_last_left)
    if_sent(near_chip_right, n_right)
    if_sent(near_chip_left, n_left)
    if_sent(near_chip_left & near_chip_right, relay_right, relay_left)
    if_sent(chip >= 1 + parity, low_early)
    if_sent(chip < chips - 2 + parity, high_early)


def per_device(
    rhs,
    ridge,
    leaf_basis,
    leaf_transfer,
    near_blocks,
    near_list,
    leaf_coupling,
    leaf_far,
    node_coupling,
    node_far,
):
    leaves, size, rank = leaf_basis.shape
    columns = rhs.shape[0]
    count = lax.axis_size("pts")
    in_hbm = pl.BlockSpec(memory_space=pltpu.HBM)
    in_vmem = pl.BlockSpec(memory_space=pltpu.VMEM)
    inner = 3 * leaves - 2
    operands = (
        rhs,
        leaf_basis,
        leaf_transfer,
        near_blocks,
        near_list,
        leaf_coupling,
        leaf_far,
        node_coupling,
        node_far,
    )
    result = pl.pallas_call(
        lambda *refs: kernel(count, *refs),
        out_shape=pltpu.VMEM((columns, leaves * size), F32),
        in_specs=[in_hbm] * len(operands),
        out_specs=in_vmem,
        scratch_shapes=[
            pltpu.VMEM((inner, columns, size), F32),
            pltpu.VMEM((2, columns, size), F32),
            pltpu.VMEM((inner, columns, rank), F32),
            pltpu.VMEM((2, columns, rank), F32),
            pltpu.VMEM((columns, rank), F32),
            pltpu.VMEM((6, columns, rank), F32),
            pltpu.VMEM((columns, rank), F32),
            pltpu.VMEM(leaf_basis.shape, F32),
            pltpu.VMEM(leaf_transfer.shape, F32),
            pltpu.VMEM(near_blocks.shape, F32),
            pltpu.VMEM(leaf_coupling.shape, F32),
            pltpu.VMEM(node_coupling.shape[1:], F32),
            pltpu.VMEM((leaves, 2, size, rank), BF16),
            pltpu.VMEM((leaves, 2, rank, rank), BF16),
            pltpu.VMEM((2, 4, size, size), BF16),
            pltpu.VMEM((6, 2, rank, rank), BF16),
            pltpu.SMEM(near_list.shape, jnp.int32),
            pltpu.SMEM(leaf_far.shape, jnp.int32),
            pltpu.SMEM(node_far.shape, jnp.int32),
            pltpu.SemaphoreType.DMA((3 * leaves + 6,)),
            pltpu.SemaphoreType.DMA((11 + 2 * leaves,)),
            pltpu.SemaphoreType.DMA((11 + 2 * leaves,)),
        ],
        compiler_params=pltpu.CompilerParams(
            collective_id=0, has_side_effects=True, vmem_limit_bytes=24 * 2**20
        ),
    )(*[pltpu.with_memory_space_constraint(value, pltpu.HBM) for value in operands])
    return result + ridge[None, :] * rhs


def solution(mesh):
    in_specs = (
        P(None, "pts"),
        P("pts"),
        P("pts", None, None),
        P("pts", None, None),
        P("pts", None, None, None),
        P("pts", None),
        P("pts", None, None, None),
        P("pts", None),
        P("pts", None, None, None),
        P("pts", None),
    )
    return jax.shard_map(
        per_device, mesh=mesh, in_specs=in_specs, out_specs=P(None, "pts"), check_vma=False
    )
```

```python
import jax
import jax.numpy as jnp
from jax import lax
from jax.experimental import pallas as pl
from jax.experimental.pallas import tpu as pltpu
from jax.sharding import PartitionSpec as P

F32 = jnp.float32
BF16 = jnp.bfloat16
MESH = pl.DeviceIdType.MESH

COLUMN = 8


def split(value):
    high = value.astype(BF16)
    low = (value - high.astype(F32)).astype(BF16)
    return high, low


def stacked(value):
    high, low = split(value)
    return jnp.concatenate([high, low], axis=0)


def halves(left, high, low, transposed=False):
    rows = left.shape[0] // 2
    dims = (((1,), (1 if transposed else 0,)), ((), ()))
    both = lax.dot_general(left, high, dims, preferred_element_type=F32)
    rest = lax.dot_general(left[:rows], low, dims, preferred_element_type=F32)
    return both[:rows] + (both[rows:] + rest)


def product(left, weight):
    return halves(left, *split(weight))


def inside(index, extent):
    return jnp.minimum(jnp.maximum(index, 0), extent - 1)


def flag(condition):
    return condition.astype(jnp.int32).astype(F32)


def kernel(
    count,
    rhs,
    basis_hbm,
    transfer_hbm,
    near_hbm,
    near_list_hbm,
    coupling_hbm,
    leaf_far_hbm,
    node_coupling_hbm,
    node_far_hbm,
    out,
    x_window,
    x_last,
    m_window,
    m_last,
    n_own,
    n_window,
    field_sum,
    basis,
    transfer,
    near,
    coupling,
    node_coupling,
    basis_parts,
    transfer_parts,
    last_parts,
    node_parts,
    near_list,
    leaf_far,
    node_far,
    load_sem,
    send_sem,
    recv_sem,
):
    leaves, size = basis.shape[:2]
    inner = 3 * leaves - 2
    me = lax.axis_index("pts")
    parity = lax.rem(me, 2)
    chip = me // 2
    chips = count // 2
    even = parity == 0
    odd = parity == 1
    has_left = me >= 1
    has_right = me < count - 1
    near_chip_left = chip >= 1
    near_chip_right = chip < chips - 1
    far_chip_left = chip >= 2
    far_chip_right = chip < chips - 2
    right = jnp.minimum(me + 1, count - 1)
    left = jnp.maximum(me - 1, 0)
    right2 = jnp.minimum(me + 2, count - 1)
    left2 = jnp.maximum(me - 2, 0)
    place = lax.rem(chip, COLUMN)
    right_first = place < 2
    relays = near_chip_left & near_chip_right
    partner = me + 1 - 2 * parity
    first = me * leaves - leaves

    def cols(l):
        return slice(l * size, (l + 1) * size)

    barrier = pltpu.get_barrier_semaphore()
    expected = 0
    for other, there in (
        (left, has_left),
        (right, has_right),
        (left2, near_chip_left),
        (right2, near_chip_right),
    ):
        expected = expected + there.astype(jnp.int32)

        @pl.when(there)
        def _(other=other):
            pl.semaphore_signal(barrier, inc=1, device_id=(other,), device_id_type=MESH)

    def load(source, target, number):
        copy = pltpu.make_async_copy(source, target, load_sem.at[number])
        copy.start()
        return copy

    for l in range(leaves):
        load(rhs.at[:, cols(l)], x_window.at[leaves - 1 + l], 0)
    basis_loads = [load(basis_hbm.at[l], basis.at[l], 1 + l) for l in range(leaves)]
    transfer_loads = [
        load(transfer_hbm.at[l], transfer.at[l], 1 + leaves + l) for l in range(leaves)
    ]
    base = 2 * leaves + 1
    list_loads = [
        load(near_list_hbm, near_list, base),
        load(leaf_far_hbm, leaf_far, base + 1),
        load(node_far_hbm, node_far, base + 2),
    ]

    pl.semaphore_wait(barrier, expected)

    def remote(source, target, number, departure, device):
        return pltpu.make_async_remote_copy(
            src_ref=source,
            dst_ref=target,
            send_sem=send_sem.at[departure],
            recv_sem=recv_sem.at[number],
            device_id=(device,),
            device_id_type=MESH,
        )

    end = leaves - 1
    x_right = [
        remote(x_window.at[end + l], x_window.at[l - 1], 0, 0, right) for l in range(end, 0, -1)
    ]
    x_left = [
        remote(x_window.at[end + l], x_window.at[2 * leaves - 1 + l], 1, 1, left)
        for l in range(end)
    ]
    low, high = x_window.at[0:end], x_window.at[2 * leaves - 1 : inner]
    x_from_left = remote(low, low, 0, 0, right)
    x_from_right = remote(high, high, 1, 1, left)
    m_right = remote(m_window.at[leaves : 2 * leaves - 1], m_window.at[0:end], 2, 0, right)
    m_left = remote(m_window.at[end : 2 * end], m_window.at[2 * leaves - 1 : inner], 3, 1, left)
    m_last_right = remote(m_window.at[end], m_last.at[0], 4, 0, right)
    m_last_left = remote(m_window.at[2 * end], m_last.at[1], 5, 1, left)
    x_last_right = remote(x_window.at[end], x_last.at[0], 6, 0, right)
    x_last_left = remote(x_window.at[2 * end], x_last.at[1], 7, 1, left)
    n_right = remote(n_own, n_window.at[2], 8, 2, right2)
    n_left = remote(n_own, n_window.at[3], 9, 3, left2)
    relay_right = remote(n_window.at[2], n_window.at[0], 10, 4, right2)
    relay_left = remote(n_window.at[3], n_window.at[5], 11, 5, left2)
    low_early = remote(n_window.at[2], n_window.at[1], 12, 6, partner)
    low_late = remote(n_window.at[0], n_window.at[1], 12, 6, partner)
    high_early = remote(n_window.at[3], n_window.at[4], 13, 7, partner)
    high_late = remote(n_window.at[5], n_window.at[4], 13, 7, partner)

    def if_start(condition, *copies):
        @pl.when(condition)
        def _():
            for copy in copies:
                copy.start()

    def if_arrived(condition, *copies):
        @pl.when(condition)
        def _():
            for copy in copies:
                copy.wait_recv()

    x_own = x_window.at[end : end + leaves]
    pltpu.make_async_copy(x_own, x_own, load_sem.at[0]).wait()
    if_start(has_right, *x_right)
    if_start(has_left, *x_left)
    node_load = load(node_coupling_hbm.at[0], node_coupling, base + 5)
    near_load = load(near_hbm, near, base + 3)
    coupling_load = load(coupling_hbm, coupling, base + 4)

    node = None
    for l in range(leaves):
        basis_loads[l].wait()
        high, low = split(basis[l])
        basis_parts[l, 0] = high
        basis_parts[l, 1] = low
        moment = halves(stacked(x_window[end + l]), high, low)
        m_window[end + l] = moment
        transfer_loads[l].wait()
        high, low = split(transfer[l])
        transfer_parts[l, 0] = high
        transfer_parts[l, 1] = low
        term = halves(stacked(moment), high, low)
        node = term if node is None else node + term
    n_own[...] = node

    if_start(near_chip_right, n_right)
    if_start(near_chip_left, n_left)
    if_start(has_right, m_right)
    if_start(has_left, m_left)

    for copy in list_loads:
        copy.wait()
    node_load.wait()
    entries = node_coupling.shape[0]
    for s, offset in enumerate((-4, -3, -2, 2, 3, 4)):
        total = None
        for k in range(entries):
            term = flag(node_far[0, k] == me + offset) * node_coupling[k]
            total = term if total is None else total + term
        node_parts[s, 0], node_parts[s, 1] = split(total)

    for l in range(leaves):
        left_parts = jnp.concatenate([basis_parts[l, 0], basis_parts[l, 1]], axis=0)
        both = halves(left_parts, transfer_parts[l, 0], transfer_parts[l, 1])
        transfer_parts[l, 0], transfer_parts[l, 1] = split(both)

    near_load.wait()
    for l in range(leaves):
        out[:, cols(l)] = product(stacked(x_window[end + l]), near[l, 0])

    def from_left():
        @pl.when(near_chip_left)
        def _():
            n_right.wait_recv()
            if_start(near_chip_right, relay_right)
            if_start(even, low_early)

        if_start(has_right, m_last_right, x_last_right)

    def from_right():
        @pl.when(near_chip_right)
        def _():
            n_left.wait_recv()
            if_start(near_chip_left, relay_left)
            if_start(odd, high_early)

        if_start(has_left, m_last_left, x_last_left)

    def in_order(one, other):
        @pl.when(right_first)
        def _():
            other()
            one()

        @pl.when(jnp.logical_not(right_first))
        def _():
            one()
            other()

    in_order(from_left, from_right)

    coupling_load.wait()
    ends = ((0, 0, first), (1, end, first + 3 * leaves - 1))
    for side, l, source in ends:
        total = flag(near_list[l, 1] == source) * near[l, 1]
        for j in range(2, near.shape[1]):
            total = total + flag(near_list[l, j] == source) * near[l, j]
        last_parts[side, 0], last_parts[side, 1] = split(total)
        total = flag(leaf_far[l, 0] == source) * coupling[l, 0]
        for k in range(1, coupling.shape[1]):
            total = total + flag(leaf_far[l, k] == source) * coupling[l, k]
        last_parts[side, 2], last_parts[side, 3] = split(total)

    def chosen(window, leaf, l):
        slot = leaf - first - 1
        value = window[inside(slot, inner)]
        if l == 0:
            value = value * flag(slot >= 0)
        if l == end:
            value = value * flag(slot < inner)
        return stacked(value)

    if_arrived(has_left, x_from_left)
    if_arrived(has_right, x_from_right)
    for l in range(leaves):
        total = out[:, cols(l)]
        for j in range(1, near.shape[1]):
            total = total + product(chosen(x_window, near_list[l, j], l), near[l, j])
        out[:, cols(l)] = total

    if_arrived(has_left, m_right)
    if_arrived(has_right, m_left)
    for l in range(leaves):
        total = None
        for k in range(coupling.shape[1]):
            term = product(chosen(m_window, leaf_far[l, k], l), coupling[l, k])
            total = term if total is None else total + term
        total = halves(stacked(total), basis_parts[l, 0], basis_parts[l, 1], True)
        out[:, cols(l)] = out[:, cols(l)] + total

    def node_term(s, there):
        value = stacked(jnp.where(there, n_window[s], 0.0))
        return halves(value, node_parts[s, 0], node_parts[s, 1])

    field_sum[...] = node_term(2, near_chip_left) + node_term(3, near_chip_right)

    def later_left():
        @pl.when(far_chip_left)
        def _():
            relay_right.wait_recv()
            if_start(odd, low_late)

    def later_right():
        @pl.when(far_chip_right)
        def _():
            relay_left.wait_recv()
            if_start(even, high_late)

    in_order(later_left, later_right)
    field_sum[...] = (
        field_sum[...] + node_term(0, far_chip_left) + node_term(5, far_chip_right)
    )

    if_arrived(has_left, m_last_right)
    if_arrived(has_right, m_last_left)

    def last(buffer, side):
        return stacked(jnp.where((has_left, has_right)[side], buffer[side], 0.0))

    for side, l in ((0, 0), (1, end)):
        total = halves(last(m_last, side), last_parts[side, 2], last_parts[side, 3])
        total = halves(stacked(total), basis_parts[l, 0], basis_parts[l, 1], True)
        out[:, cols(l)] = out[:, cols(l)] + total

    low_there = chip >= 2 - parity
    high_there = chip < chips - 1 - parity
    if_arrived(low_there, low_early)
    if_arrived(high_there, high_early)
    field = stacked(field_sum[...] + node_term(1, low_there) + node_term(4, high_there))
    for l in range(leaves):
        term = halves(field, transfer_parts[l, 0], transfer_parts[l, 1], True)
        out[:, cols(l)] = out[:, cols(l)] + term

    def if_sent(condition, copy):
        @pl.when(condition)
        def _():
            copy.wait_send()

    everything = m_window.at[0 : 2 * leaves]
    if_sent(has_right, remote(everything, everything, 0, 0, right))
    if_sent(has_left, remote(everything, everything, 0, 1, left))
    if_sent(near_chip_right, n_right)
    if_sent(near_chip_left, n_left)
    if_sent(relays, relay_right)
    if_sent(relays, relay_left)
    if_sent(chip >= 1 + parity, low_early)
    if_sent(chip < chips - 2 + parity, high_early)

    if_arrived(has_left, x_last_right)
    if_arrived(has_right, x_last_left)
    for side, l in ((0, 0), (1, end)):
        parts = last_parts[side, 0], last_parts[side, 1]
        out[:, cols(l)] = out[:, cols(l)] + halves(last(x_last, side), *parts)


def per_device(
    rhs,
    ridge,
    leaf_basis,
    leaf_transfer,
    near_blocks,
    near_list,
    leaf_coupling,
    leaf_far,
    node_coupling,
    node_far,
):
    leaves, size, rank = leaf_basis.shape
    columns = rhs.shape[0]
    count = lax.axis_size("pts")
    in_hbm = pl.BlockSpec(memory_space=pltpu.HBM)
    in_vmem = pl.BlockSpec(memory_space=pltpu.VMEM)
    inner = 3 * leaves - 2
    operands = (
        rhs,
        leaf_basis,
        leaf_transfer,
        near_blocks,
        near_list,
        leaf_coupling,
        leaf_far,
        node_coupling,
        node_far,
    )
    result = pl.pallas_call(
        lambda *refs: kernel(count, *refs),
        out_shape=pltpu.VMEM((columns, leaves * size), F32),
        in_specs=[in_hbm] * len(operands),
        out_specs=in_vmem,
        scratch_shapes=[
            pltpu.VMEM((inner, columns, size), F32),
            pltpu.VMEM((2, columns, size), F32),
            pltpu.VMEM((inner, columns, rank), F32),
            pltpu.VMEM((2, columns, rank), F32),
            pltpu.VMEM((columns, rank), F32),
            pltpu.VMEM((6, columns, rank), F32),
            pltpu.VMEM((columns, rank), F32),
            pltpu.VMEM(leaf_basis.shape, F32),
            pltpu.VMEM(leaf_transfer.shape, F32),
            pltpu.VMEM(near_blocks.shape, F32),
            pltpu.VMEM(leaf_coupling.shape, F32),
            pltpu.VMEM(node_coupling.shape[1:], F32),
            pltpu.VMEM((leaves, 2, size, rank), BF16),
            pltpu.VMEM((leaves, 2, rank, rank), BF16),
            pltpu.VMEM((2, 4, size, size), BF16),
            pltpu.VMEM((6, 2, rank, rank), BF16),
            pltpu.SMEM(near_list.shape, jnp.int32),
            pltpu.SMEM(leaf_far.shape, jnp.int32),
            pltpu.SMEM(node_far.shape, jnp.int32),
            pltpu.SemaphoreType.DMA((2 * leaves + 7,)),
            pltpu.SemaphoreType.DMA((8,)),
            pltpu.SemaphoreType.DMA((14,)),
        ],
        compiler_params=pltpu.CompilerParams(
            collective_id=0, has_side_effects=True, vmem_limit_bytes=24 * 2**20
        ),
    )(*[pltpu.with_memory_space_constraint(value, pltpu.HBM) for value in operands])
    return result + ridge[None, :] * rhs


def solution(mesh):
    in_specs = (
        P(None, "pts"),
        P("pts"),
        P("pts", None, None),
        P("pts", None, None),
        P("pts", None, None, None),
        P("pts", None),
        P("pts", None, None, None),
        P("pts", None),
        P("pts", None, None, None),
        P("pts", None),
    )
    return jax.shard_map(
        per_device, mesh=mesh, in_specs=in_specs, out_specs=P(None, "pts"), check_vma=False
    )
```

```python
import jax
import jax.numpy as jnp
from jax import lax
from jax.experimental import pallas as pl
from jax.experimental.pallas import tpu as pltpu
from jax.sharding import PartitionSpec as P

F32 = jnp.float32
BF16 = jnp.bfloat16
MESH = pl.DeviceIdType.MESH

COLUMN = 8


def split(value):
    high = value.astype(BF16)
    low = (value - high.astype(F32)).astype(BF16)
    return high, low


def stacked(value):
    high, low = split(value)
    return jnp.concatenate([high, low], axis=0)


def halves(left, high, low, transposed=False):
    rows = left.shape[0] // 2
    dims = (((1,), (1 if transposed else 0,)), ((), ()))
    both = lax.dot_general(left, high, dims, preferred_element_type=F32)
    rest = lax.dot_general(left[:rows], low, dims, preferred_element_type=F32)
    return both[:rows] + (both[rows:] + rest)


def product(left, weight):
    return halves(left, *split(weight))


def inside(index, extent):
    return jnp.minimum(jnp.maximum(index, 0), extent - 1)


def flag(condition):
    return condition.astype(jnp.int32).astype(F32)


def kernel(
    count,
    rhs,
    basis_hbm,
    transfer_hbm,
    near_hbm,
    near_list_hbm,
    coupling_hbm,
    leaf_far_hbm,
    node_coupling_hbm,
    node_far_hbm,
    out,
    x_window,
    x_last,
    m_window,
    m_last,
    n_own,
    n_window,
    field_sum,
    basis,
    transfer,
    near,
    coupling,
    node_coupling,
    basis_parts,
    transfer_parts,
    last_parts,
    node_parts,
    coupling_parts,
    near_list,
    leaf_far,
    node_far,
    load_sem,
    send_sem,
    recv_sem,
):
    leaves, size = basis.shape[:2]
    inner = 3 * leaves - 2
    me = lax.axis_index("pts")
    parity = lax.rem(me, 2)
    chip = me // 2
    chips = count // 2
    even = parity == 0
    odd = parity == 1
    has_left = me >= 1
    has_right = me < count - 1
    near_chip_left = chip >= 1
    near_chip_right = chip < chips - 1
    far_chip_left = chip >= 2
    far_chip_right = chip < chips - 2
    right = jnp.minimum(me + 1, count - 1)
    left = jnp.maximum(me - 1, 0)
    right2 = jnp.minimum(me + 2, count - 1)
    left2 = jnp.maximum(me - 2, 0)
    place = lax.rem(chip, COLUMN)
    right_first = place < 2
    relays = near_chip_left & near_chip_right
    partner = me + 1 - 2 * parity
    first = me * leaves - leaves

    def cols(l):
        return slice(l * size, (l + 1) * size)

    barrier = pltpu.get_barrier_semaphore()
    expected = 0
    for other, there in (
        (left, has_left),
        (right, has_right),
        (left2, near_chip_left),
        (right2, near_chip_right),
    ):
        expected = expected + there.astype(jnp.int32)

        @pl.when(there)
        def _(other=other):
            pl.semaphore_signal(barrier, inc=1, device_id=(other,), device_id_type=MESH)

    def load(source, target, number):
        copy = pltpu.make_async_copy(source, target, load_sem.at[number])
        copy.start()
        return copy

    for l in range(leaves):
        load(rhs.at[:, cols(l)], x_window.at[leaves - 1 + l], 0)
    basis_loads = [load(basis_hbm.at[l], basis.at[l], 1 + l) for l in range(leaves)]
    transfer_loads = [
        load(transfer_hbm.at[l], transfer.at[l], 1 + leaves + l) for l in range(leaves)
    ]
    base = 2 * leaves + 1
    list_loads = [
        load(near_list_hbm, near_list, base),
        load(leaf_far_hbm, leaf_far, base + 1),
        load(node_far_hbm, node_far, base + 2),
    ]

    pl.semaphore_wait(barrier, expected)

    def remote(source, target, number, departure, device):
        return pltpu.make_async_remote_copy(
            src_ref=source,
            dst_ref=target,
            send_sem=send_sem.at[departure],
            recv_sem=recv_sem.at[number],
            device_id=(device,),
            device_id_type=MESH,
        )

    end = leaves - 1
    x_right = [
        remote(x_window.at[end + l], x_window.at[l - 1], 0, 0, right) for l in range(end, 0, -1)
    ]
    x_left = [
        remote(x_window.at[end + l], x_window.at[2 * leaves - 1 + l], 1, 1, left)
        for l in range(end)
    ]
    low, high = x_window.at[0:end], x_window.at[2 * leaves - 1 : inner]
    x_from_left = remote(low, low, 0, 0, right)
    x_from_right = remote(high, high, 1, 1, left)
    m_right = remote(m_window.at[leaves : 2 * leaves - 1], m_window.at[0:end], 2, 0, right)
    m_left = remote(m_window.at[end : 2 * end], m_window.at[2 * leaves - 1 : inner], 3, 1, left)
    m_last_right = remote(m_window.at[end], m_last.at[0], 4, 0, right)
    m_last_left = remote(m_window.at[2 * end], m_last.at[1], 5, 1, left)
    x_last_right = remote(x_window.at[end], x_last.at[0], 6, 0, right)
    x_last_left = remote(x_window.at[2 * end], x_last.at[1], 7, 1, left)
    n_right = remote(n_own, n_window.at[2], 8, 2, right2)
    n_left = remote(n_own, n_window.at[3], 9, 3, left2)
    relay_right = remote(n_window.at[2], n_window.at[0], 10, 4, right2)
    relay_left = remote(n_window.at[3], n_window.at[5], 11, 5, left2)
    low_early = remote(n_window.at[2], n_window.at[1], 12, 6, partner)
    low_late = remote(n_window.at[0], n_window.at[1], 12, 6, partner)
    high_early = remote(n_window.at[3], n_window.at[4], 13, 7, partner)
    high_late = remote(n_window.at[5], n_window.at[4], 13, 7, partner)

    def if_start(condition, *copies):
        @pl.when(condition)
        def _():
            for copy in copies:
                copy.start()

    def if_arrived(condition, *copies):
        @pl.when(condition)
        def _():
            for copy in copies:
                copy.wait_recv()

    x_own = x_window.at[end : end + leaves]
    pltpu.make_async_copy(x_own, x_own, load_sem.at[0]).wait()
    if_start(has_right, *x_right[:2])
    if_start(has_left, *x_left[:2])
    node_load = load(node_coupling_hbm.at[0], node_coupling, base + 5)
    near_load = load(near_hbm, near, base + 3)
    coupling_load = load(coupling_hbm, coupling, base + 4)

    node = None
    for l in range(leaves):
        basis_loads[l].wait()
        high, low = split(basis[l])
        basis_parts[l, 0] = high
        basis_parts[l, 1] = low
        moment = halves(stacked(x_window[end + l]), high, low)
        m_window[end + l] = moment
        transfer_loads[l].wait()
        high, low = split(transfer[l])
        transfer_parts[l, 0] = high
        transfer_parts[l, 1] = low
        term = halves(stacked(moment), high, low)
        node = term if node is None else node + term
    n_own[...] = node

    if_start(near_chip_right, n_right)
    if_start(near_chip_left, n_left)
    if_start(has_right, x_right[2], m_right)
    if_start(has_left, x_left[2], m_left)

    for copy in list_loads:
        copy.wait()
    node_load.wait()
    entries = node_coupling.shape[0]
    for s, offset in enumerate((-4, -3, -2, 2, 3, 4)):
        total = None
        for k in range(entries):
            term = flag(node_far[0, k] == me + offset) * node_coupling[k]
            total = term if total is None else total + term
        node_parts[s, 0], node_parts[s, 1] = split(total)

    for l in range(leaves):
        left_parts = jnp.concatenate([basis_parts[l, 0], basis_parts[l, 1]], axis=0)
        both = halves(left_parts, transfer_parts[l, 0], transfer_parts[l, 1])
        transfer_parts[l, 0], transfer_parts[l, 1] = split(both)

    near_load.wait()
    for l in range(leaves):
        out[:, cols(l)] = product(stacked(x_window[end + l]), near[l, 0])

    def from_left():
        @pl.when(near_chip_left)
        def _():
            n_right.wait_recv()
            if_start(near_chip_right, relay_right)
            if_start(even, low_early)

        if_start(has_right, m_last_right, x_last_right)

    def from_right():
        @pl.when(near_chip_right)
        def _():
            n_left.wait_recv()
            if_start(near_chip_left, relay_left)
            if_start(odd, high_early)

        if_start(has_left, m_last_left, x_last_left)

    def in_order(one, other):
        @pl.when(right_first)
        def _():
            other()
            one()

        @pl.when(jnp.logical_not(right_first))
        def _():
            one()
            other()

    in_order(from_left, from_right)

    coupling_load.wait()
    ends = ((0, 0, first), (1, end, first + 3 * leaves - 1))
    for side, l, source in ends:
        total = flag(near_list[l, 1] == source) * near[l, 1]
        for j in range(2, near.shape[1]):
            total = total + flag(near_list[l, j] == source) * near[l, j]
        last_parts[side, 0], last_parts[side, 1] = split(total)
        total = flag(leaf_far[l, 0] == source) * coupling[l, 0]
        for k in range(1, coupling.shape[1]):
            total = total + flag(leaf_far[l, k] == source) * coupling[l, k]
        last_parts[side, 2], last_parts[side, 3] = split(total)

    def chosen(window, leaf, l):
        slot = leaf - first - 1
        value = window[inside(slot, inner)]
        if l == 0:
            value = value * flag(slot >= 0)
        if l == end:
            value = value * flag(slot < inner)
        return stacked(value)

    for l in range(leaves):
        for k in range(coupling.shape[1]):
            coupling_parts[l, k, 0], coupling_parts[l, k, 1] = split(coupling[l, k])

    if_arrived(has_left, x_from_left)
    if_arrived(has_right, x_from_right)
    for l in range(leaves):
        total = out[:, cols(l)]
        for j in range(1, near.shape[1]):
            total = total + product(chosen(x_window, near_list[l, j], l), near[l, j])
        out[:, cols(l)] = total

    if_arrived(has_left, m_right)
    if_arrived(has_right, m_left)
    for l in range(leaves):
        total = None
        for k in range(coupling.shape[1]):
            parts = coupling_parts[l, k, 0], coupling_parts[l, k, 1]
            term = halves(chosen(m_window, leaf_far[l, k], l), *parts)
            total = term if total is None else total + term
        total = halves(stacked(total), basis_parts[l, 0], basis_parts[l, 1], True)
        out[:, cols(l)] = out[:, cols(l)] + total

    def node_term(s, there):
        value = stacked(jnp.where(there, n_window[s], 0.0))
        return halves(value, node_parts[s, 0], node_parts[s, 1])

    field_sum[...] = node_term(2, near_chip_left) + node_term(3, near_chip_right)

    def later_left():
        @pl.when(far_chip_left)
        def _():
            relay_right.wait_recv()
            if_start(odd, low_late)

    def later_right():
        @pl.when(far_chip_right)
        def _():
            relay_left.wait_recv()
            if_start(even, high_late)

    in_order(later_left, later_right)
    field_sum[...] = (
        field_sum[...] + node_term(0, far_chip_left) + node_term(5, far_chip_right)
    )

    if_arrived(has_left, m_last_right)
    if_arrived(has_right, m_last_left)

    def last(buffer, side):
        return stacked(jnp.where((has_left, has_right)[side], buffer[side], 0.0))

    for side, l in ((0, 0), (1, end)):
        total = halves(last(m_last, side), last_parts[side, 2], last_parts[side, 3])
        total = halves(stacked(total), basis_parts[l, 0], basis_parts[l, 1], True)
        out[:, cols(l)] = out[:, cols(l)] + total

    low_there = chip >= 2 - parity
    high_there = chip < chips - 1 - parity
    if_arrived(low_there, low_early)
    if_arrived(high_there, high_early)
    field = stacked(field_sum[...] + node_term(1, low_there) + node_term(4, high_there))
    for l in range(leaves):
        term = halves(field, transfer_parts[l, 0], transfer_parts[l, 1], True)
        out[:, cols(l)] = out[:, cols(l)] + term

    def if_sent(condition, copy):
        @pl.when(condition)
        def _():
            copy.wait_send()

    everything = m_window.at[0 : 2 * leaves]
    if_sent(has_right, remote(everything, everything, 0, 0, right))
    if_sent(has_left, remote(everything, everything, 0, 1, left))
    if_sent(near_chip_right, n_right)
    if_sent(near_chip_left, n_left)
    if_sent(relays, relay_right)
    if_sent(relays, relay_left)
    if_sent(chip >= 1 + parity, low_early)
    if_sent(chip < chips - 2 + parity, high_early)

    if_arrived(has_left, x_last_right)
    if_arrived(has_right, x_last_left)
    for side, l in ((0, 0), (1, end)):
        parts = last_parts[side, 0], last_parts[side, 1]
        out[:, cols(l)] = out[:, cols(l)] + halves(last(x_last, side), *parts)


def per_device(
    rhs,
    ridge,
    leaf_basis,
    leaf_transfer,
    near_blocks,
    near_list,
    leaf_coupling,
    leaf_far,
    node_coupling,
    node_far,
):
    leaves, size, rank = leaf_basis.shape
    columns = rhs.shape[0]
    count = lax.axis_size("pts")
    in_hbm = pl.BlockSpec(memory_space=pltpu.HBM)
    in_vmem = pl.BlockSpec(memory_space=pltpu.VMEM)
    inner = 3 * leaves - 2
    operands = (
        rhs,
        leaf_basis,
        leaf_transfer,
        near_blocks,
        near_list,
        leaf_coupling,
        leaf_far,
        node_coupling,
        node_far,
    )
    result = pl.pallas_call(
        lambda *refs: kernel(count, *refs),
        out_shape=pltpu.VMEM((columns, leaves * size), F32),
        in_specs=[in_hbm] * len(operands),
        out_specs=in_vmem,
        scratch_shapes=[
            pltpu.VMEM((inner, columns, size), F32),
            pltpu.VMEM((2, columns, size), F32),
            pltpu.VMEM((inner, columns, rank), F32),
            pltpu.VMEM((2, columns, rank), F32),
            pltpu.VMEM((columns, rank), F32),
            pltpu.VMEM((6, columns, rank), F32),
            pltpu.VMEM((columns, rank), F32),
            pltpu.VMEM(leaf_basis.shape, F32),
            pltpu.VMEM(leaf_transfer.shape, F32),
            pltpu.VMEM(near_blocks.shape, F32),
            pltpu.VMEM(leaf_coupling.shape, F32),
            pltpu.VMEM(node_coupling.shape[1:], F32),
            pltpu.VMEM((leaves, 2, size, rank), BF16),
            pltpu.VMEM((leaves, 2, rank, rank), BF16),
            pltpu.VMEM((2, 4, size, size), BF16),
            pltpu.VMEM((6, 2, rank, rank), BF16),
            pltpu.VMEM(leaf_coupling.shape[:2] + (2, rank, rank), BF16),
            pltpu.SMEM(near_list.shape, jnp.int32),
            pltpu.SMEM(leaf_far.shape, jnp.int32),
            pltpu.SMEM(node_far.shape, jnp.int32),
            pltpu.SemaphoreType.DMA((2 * leaves + 7,)),
            pltpu.SemaphoreType.DMA((8,)),
            pltpu.SemaphoreType.DMA((14,)),
        ],
        compiler_params=pltpu.CompilerParams(
            collective_id=0, has_side_effects=True, vmem_limit_bytes=30 * 2**20
        ),
    )(*[pltpu.with_memory_space_constraint(value, pltpu.HBM) for value in operands])
    return result + ridge[None, :] * rhs


def solution(mesh):
    in_specs = (
        P(None, "pts"),
        P("pts"),
        P("pts", None, None),
        P("pts", None, None),
        P("pts", None, None, None),
        P("pts", None),
        P("pts", None, None, None),
        P("pts", None),
        P("pts", None, None, None),
        P("pts", None),
    )
    return jax.shard_map(
        per_device, mesh=mesh, in_specs=in_specs, out_specs=P(None, "pts"), check_vma=False
    )
```

```python
import jax
import jax.numpy as jnp
from jax import lax
from jax.experimental import pallas as pl
from jax.experimental.pallas import tpu as pltpu
from jax.sharding import PartitionSpec as P

F32 = jnp.float32
BF16 = jnp.bfloat16
MESH = pl.DeviceIdType.MESH

COLUMN = 8


def split(value):
    high = value.astype(BF16)
    low = (value - high.astype(F32)).astype(BF16)
    return high, low


def stacked(value):
    high, low = split(value)
    return jnp.concatenate([high, low], axis=0)


def halves(left, high, low, transposed=False):
    rows = left.shape[0] // 2
    dims = (((1,), (1 if transposed else 0,)), ((), ()))
    both = lax.dot_general(left, high, dims, preferred_element_type=F32)
    rest = lax.dot_general(left[:rows], low, dims, preferred_element_type=F32)
    return both[:rows] + (both[rows:] + rest)


def product(left, weight):
    return halves(left, *split(weight))


def inside(index, extent):
    return jnp.minimum(jnp.maximum(index, 0), extent - 1)


def flag(condition):
    return condition.astype(jnp.int32).astype(F32)


def kernel(
    count,
    rhs,
    basis_hbm,
    transfer_hbm,
    near_hbm,
    near_list_hbm,
    coupling_hbm,
    leaf_far_hbm,
    node_coupling_hbm,
    node_far_hbm,
    out,
    x_window,
    x_last,
    m_window,
    m_last,
    n_own,
    n_window,
    field_sum,
    basis,
    transfer,
    near,
    coupling,
    node_coupling,
    basis_parts,
    transfer_parts,
    last_parts,
    node_parts,
    coupling_parts,
    near_list,
    leaf_far,
    node_far,
    load_sem,
    send_sem,
    recv_sem,
):
    leaves, size = basis.shape[:2]
    inner = 3 * leaves - 2
    me = lax.axis_index("pts")
    parity = lax.rem(me, 2)
    chip = me // 2
    chips = count // 2
    even = parity == 0
    odd = parity == 1
    has_left = me >= 1
    has_right = me < count - 1
    near_chip_left = chip >= 1
    near_chip_right = chip < chips - 1
    far_chip_left = chip >= 2
    far_chip_right = chip < chips - 2
    right = jnp.minimum(me + 1, count - 1)
    left = jnp.maximum(me - 1, 0)
    right2 = jnp.minimum(me + 2, count - 1)
    left2 = jnp.maximum(me - 2, 0)
    place = lax.rem(chip, COLUMN)
    right_first = place < 2
    relays = near_chip_left & near_chip_right
    partner = me + 1 - 2 * parity
    first = me * leaves - leaves

    def cols(l):
        return slice(l * size, (l + 1) * size)

    barrier = pltpu.get_barrier_semaphore()
    expected = 0
    for other, there in (
        (left, has_left),
        (right, has_right),
        (left2, near_chip_left),
        (right2, near_chip_right),
    ):
        expected = expected + there.astype(jnp.int32)

        @pl.when(there)
        def _(other=other):
            pl.semaphore_signal(barrier, inc=1, device_id=(other,), device_id_type=MESH)

    def load(source, target, number):
        copy = pltpu.make_async_copy(source, target, load_sem.at[number])
        copy.start()
        return copy

    for l in range(leaves):
        load(rhs.at[:, cols(l)], x_window.at[leaves - 1 + l], 0)
    basis_loads = [load(basis_hbm.at[l], basis.at[l], 1 + l) for l in range(leaves)]
    transfer_load = load(transfer_hbm, transfer, 1 + leaves)
    base = leaves + 2
    list_loads = [
        load(near_list_hbm, near_list, base),
        load(leaf_far_hbm, leaf_far, base + 1),
        load(node_far_hbm, node_far, base + 2),
    ]

    pl.semaphore_wait(barrier, expected)

    def remote(source, target, number, departure, device):
        return pltpu.make_async_remote_copy(
            src_ref=source,
            dst_ref=target,
            send_sem=send_sem.at[departure],
            recv_sem=recv_sem.at[number],
            device_id=(device,),
            device_id_type=MESH,
        )

    end = leaves - 1
    x_right = [
        remote(x_window.at[end + l], x_window.at[l - 1], 0, 0, right) for l in range(end, 0, -1)
    ]
    x_left = [
        remote(x_window.at[end + l], x_window.at[2 * leaves - 1 + l], 1, 1, left)
        for l in range(end)
    ]
    low, high = x_window.at[0:end], x_window.at[2 * leaves - 1 : inner]
    x_from_left = remote(low, low, 0, 0, right)
    x_from_right = remote(high, high, 1, 1, left)
    m_right = remote(m_window.at[leaves : 2 * leaves - 1], m_window.at[0:end], 2, 0, right)
    m_left = remote(m_window.at[end : 2 * end], m_window.at[2 * leaves - 1 : inner], 3, 1, left)
    m_last_right = remote(m_window.at[end], m_last.at[0], 4, 0, right)
    m_last_left = remote(m_window.at[2 * end], m_last.at[1], 5, 1, left)
    x_last_right = remote(x_window.at[end], x_last.at[0], 6, 0, right)
    x_last_left = remote(x_window.at[2 * end], x_last.at[1], 7, 1, left)
    n_right = remote(n_own, n_window.at[2], 8, 2, right2)
    n_left = remote(n_own, n_window.at[3], 9, 3, left2)
    relay_right = remote(n_window.at[2], n_window.at[0], 10, 4, right2)
    relay_left = remote(n_window.at[3], n_window.at[5], 11, 5, left2)
    low_early = remote(n_window.at[2], n_window.at[1], 12, 6, partner)
    low_late = remote(n_window.at[0], n_window.at[1], 12, 6, partner)
    high_early = remote(n_window.at[3], n_window.at[4], 13, 7, partner)
    high_late = remote(n_window.at[5], n_window.at[4], 13, 7, partner)

    def if_start(condition, *copies):
        @pl.when(condition)
        def _():
            for copy in copies:
                copy.start()

    def if_arrived(condition, *copies):
        @pl.when(condition)
        def _():
            for copy in copies:
                copy.wait_recv()

    x_own = x_window.at[end : end + leaves]
    pltpu.make_async_copy(x_own, x_own, load_sem.at[0]).wait()
    if_start(has_right, *x_right[:2])
    if_start(has_left, *x_left[:2])
    node_load = load(node_coupling_hbm.at[0], node_coupling, base + 5)
    near_load = load(near_hbm, near, base + 3)
    coupling_load = load(coupling_hbm, coupling, base + 4)

    node = None
    for l in range(leaves):
        basis_loads[l].wait()
        high, low = split(basis[l])
        basis_parts[l, 0] = high
        basis_parts[l, 1] = low
        moment = halves(stacked(x_window[end + l]), high, low)
        m_window[end + l] = moment
        if l == 0:
            transfer_load.wait()
        high, low = split(transfer[l])
        transfer_parts[l, 0] = high
        transfer_parts[l, 1] = low
        term = halves(stacked(moment), high, low)
        node = term if node is None else node + term
    n_own[...] = node

    if_start(near_chip_right, n_right)
    if_start(near_chip_left, n_left)
    if_start(has_right, x_right[2], m_right)
    if_start(has_left, x_left[2], m_left)

    for copy in list_loads:
        copy.wait()
    node_load.wait()
    entries = node_coupling.shape[0]
    for s, offset in enumerate((-4, -3, -2, 2, 3, 4)):
        total = None
        for k in range(entries):
            term = flag(node_far[0, k] == me + offset) * node_coupling[k]
            total = term if total is None else total + term
        node_parts[s, 0], node_parts[s, 1] = split(total)

    for l in range(leaves):
        left_parts = jnp.concatenate([basis_parts[l, 0], basis_parts[l, 1]], axis=0)
        both = halves(left_parts, transfer_parts[l, 0], transfer_parts[l, 1])
        transfer_parts[l, 0], transfer_parts[l, 1] = split(both)

    near_load.wait()
    for l in range(leaves):
        out[:, cols(l)] = product(stacked(x_window[end + l]), near[l, 0])

    def from_left():
        @pl.when(near_chip_left)
        def _():
            n_right.wait_recv()
            if_start(near_chip_right, relay_right)
            if_start(even, low_early)

        if_start(has_right, m_last_right, x_last_right)

    def from_right():
        @pl.when(near_chip_right)
        def _():
            n_left.wait_recv()
            if_start(near_chip_left, relay_left)
            if_start(odd, high_early)

        if_start(has_left, m_last_left, x_last_left)

    def in_order(one, other):
        @pl.when(right_first)
        def _():
            other()
            one()

        @pl.when(jnp.logical_not(right_first))
        def _():
            one()
            other()

    in_order(from_left, from_right)

    coupling_load.wait()
    ends = ((0, 0, first), (1, end, first + 3 * leaves - 1))
    for side, l, source in ends:
        total = flag(near_list[l, 1] == source) * near[l, 1]
        for j in range(2, near.shape[1]):
            total = total + flag(near_list[l, j] == source) * near[l, j]
        last_parts[side, 0], last_parts[side, 1] = split(total)
        total = flag(leaf_far[l, 0] == source) * coupling[l, 0]
        for k in range(1, coupling.shape[1]):
            total = total + flag(leaf_far[l, k] == source) * coupling[l, k]
        last_parts[side, 2], last_parts[side, 3] = split(total)

    def chosen(window, leaf, l):
        slot = leaf - first - 1
        value = window[inside(slot, inner)]
        if l == 0:
            value = value * flag(slot >= 0)
        if l == end:
            value = value * flag(slot < inner)
        return stacked(value)

    for l in range(leaves):
        for k in range(coupling.shape[1]):
            coupling_parts[l, k, 0], coupling_parts[l, k, 1] = split(coupling[l, k])

    if_arrived(has_left, x_from_left)
    if_arrived(has_right, x_from_right)
    for l in range(leaves):
        total = out[:, cols(l)]
        for j in range(1, near.shape[1]):
            total = total + product(chosen(x_window, near_list[l, j], l), near[l, j])
        out[:, cols(l)] = total

    if_arrived(has_left, m_right)
    if_arrived(has_right, m_left)
    for l in range(leaves):
        total = None
        for k in range(coupling.shape[1]):
            parts = coupling_parts[l, k, 0], coupling_parts[l, k, 1]
            term = halves(chosen(m_window, leaf_far[l, k], l), *parts)
            total = term if total is None else total + term
        total = halves(stacked(total), basis_parts[l, 0], basis_parts[l, 1], True)
        out[:, cols(l)] = out[:, cols(l)] + total

    def node_term(s, there):
        value = stacked(jnp.where(there, n_window[s], 0.0))
        return halves(value, node_parts[s, 0], node_parts[s, 1])

    field_sum[...] = node_term(2, near_chip_left) + node_term(3, near_chip_right)

    def later_left():
        @pl.when(far_chip_left)
        def _():
            relay_right.wait_recv()
            if_start(odd, low_late)

    def later_right():
        @pl.when(far_chip_right)
        def _():
            relay_left.wait_recv()
            if_start(even, high_late)

    in_order(later_left, later_right)
    field_sum[...] = (
        field_sum[...] + node_term(0, far_chip_left) + node_term(5, far_chip_right)
    )

    if_arrived(has_left, m_last_right)
    if_arrived(has_right, m_last_left)

    def last(buffer, side):
        return stacked(jnp.where((has_left, has_right)[side], buffer[side], 0.0))

    for side, l in ((0, 0), (1, end)):
        total = halves(last(m_last, side), last_parts[side, 2], last_parts[side, 3])
        total = halves(stacked(total), basis_parts[l, 0], basis_parts[l, 1], True)
        out[:, cols(l)] = out[:, cols(l)] + total

    low_there = chip >= 2 - parity
    high_there = chip < chips - 1 - parity
    if_arrived(low_there, low_early)
    if_arrived(high_there, high_early)
    field = stacked(field_sum[...] + node_term(1, low_there) + node_term(4, high_there))
    for l in range(leaves):
        term = halves(field, transfer_parts[l, 0], transfer_parts[l, 1], True)
        out[:, cols(l)] = out[:, cols(l)] + term

    def if_sent(condition, copy):
        @pl.when(condition)
        def _():
            copy.wait_send()

    everything = m_window.at[0 : 2 * leaves]
    if_sent(has_right, remote(everything, everything, 0, 0, right))
    if_sent(has_left, remote(everything, everything, 0, 1, left))
    if_sent(near_chip_right, n_right)
    if_sent(near_chip_left, n_left)
    if_sent(relays, relay_right)
    if_sent(relays, relay_left)
    if_sent(chip >= 1 + parity, low_early)
    if_sent(chip < chips - 2 + parity, high_early)

    if_arrived(has_left, x_last_right)
    if_arrived(has_right, x_last_left)
    for side, l in ((0, 0), (1, end)):
        parts = last_parts[side, 0], last_parts[side, 1]
        out[:, cols(l)] = out[:, cols(l)] + halves(last(x_last, side), *parts)


def per_device(
    rhs,
    ridge,
    leaf_basis,
    leaf_transfer,
    near_blocks,
    near_list,
    leaf_coupling,
    leaf_far,
    node_coupling,
    node_far,
):
    leaves, size, rank = leaf_basis.shape
    columns = rhs.shape[0]
    count = lax.axis_size("pts")
    in_hbm = pl.BlockSpec(memory_space=pltpu.HBM)
    in_vmem = pl.BlockSpec(memory_space=pltpu.VMEM)
    inner = 3 * leaves - 2
    operands = (
        rhs,
        leaf_basis,
        leaf_transfer,
        near_blocks,
        near_list,
        leaf_coupling,
        leaf_far,
        node_coupling,
        node_far,
    )
    result = pl.pallas_call(
        lambda *refs: kernel(count, *refs),
        out_shape=pltpu.VMEM((columns, leaves * size), F32),
        in_specs=[in_hbm] * len(operands),
        out_specs=in_vmem,
        scratch_shapes=[
            pltpu.VMEM((inner, columns, size), F32),
            pltpu.VMEM((2, columns, size), F32),
            pltpu.VMEM((inner, columns, rank), F32),
            pltpu.VMEM((2, columns, rank), F32),
            pltpu.VMEM((columns, rank), F32),
            pltpu.VMEM((6, columns, rank), F32),
            pltpu.VMEM((columns, rank), F32),
            pltpu.VMEM(leaf_basis.shape, F32),
            pltpu.VMEM(leaf_transfer.shape, F32),
            pltpu.VMEM(near_blocks.shape, F32),
            pltpu.VMEM(leaf_coupling.shape, F32),
            pltpu.VMEM(node_coupling.shape[1:], F32),
            pltpu.VMEM((leaves, 2, size, rank), BF16),
            pltpu.VMEM((leaves, 2, rank, rank), BF16),
            pltpu.VMEM((2, 4, size, size), BF16),
            pltpu.VMEM((6, 2, rank, rank), BF16),
            pltpu.VMEM(leaf_coupling.shape[:2] + (2, rank, rank), BF16),
            pltpu.SMEM(near_list.shape, jnp.int32),
            pltpu.SMEM(leaf_far.shape, jnp.int32),
            pltpu.SMEM(node_far.shape, jnp.int32),
            pltpu.SemaphoreType.DMA((leaves + 8,)),
            pltpu.SemaphoreType.DMA((8,)),
            pltpu.SemaphoreType.DMA((14,)),
        ],
        compiler_params=pltpu.CompilerParams(
            collective_id=0, has_side_effects=True, vmem_limit_bytes=30 * 2**20
        ),
    )(*[pltpu.with_memory_space_constraint(value, pltpu.HBM) for value in operands])
    return result + ridge[None, :] * rhs


def solution(mesh):
    in_specs = (
        P(None, "pts"),
        P("pts"),
        P("pts", None, None),
        P("pts", None, None),
        P("pts", None, None, None),
        P("pts", None),
        P("pts", None, None, None),
        P("pts", None),
        P("pts", None, None, None),
        P("pts", None),
    )
    return jax.shard_map(
        per_device, mesh=mesh, in_specs=in_specs, out_specs=P(None, "pts"), check_vma=False
    )
```
